1024 devices in a mesh: chan: 32 (over y, z_lo), ctx: 32 (over z_hi, x, core).
Axes of the slice: x: 4, y: 4, z: 32 (z_hi: 4, z_lo: 8; z = z_hi * 8 + z_lo), core: 2. Of those that a mesh axis runs over, the one named last changes fastest.
Arguments:
- key_proj: bfloat16 [32768, 4096], P('ctx', 'chan'), may hold values from -6 to 6
- value_proj: bfloat16 [32768, 4096], P('ctx', 'chan'), may hold values from -6 to 6
- query_proj: bfloat16 [32768, 4096], P('ctx', 'chan'), may hold values from -6 to 6
- short_filter: bfloat16 [3, 3, 4096], P(None, None, 'chan'), may hold values from -3.5 to 3.5
- decay_rate: float32 [16, 4096], P(None, 'chan'), may hold values from 1.5258789e-05 to 0.05
- residue: float32 [16, 4096], P(None, 'chan'), may hold values from -0.03 to 0.03
- skip_gain: float32 [4096], P('chan'), may hold values from -1 to 1
- out_weight: bfloat16 [4096, 4096], P('chan'), may hold values from -0.1875 to 0.1875
Outputs:
- block_out: bfloat16 [32768, 4096], P('ctx', 'chan')
The draws below stay inside these ranges and needn't reach their ends.
All inputs are finite; a program needn't handle non-finite values.
Results may differ from the reference program's by a relative error of at most 0.023.
Values may be sent and summed in bfloat16 or wider, within the bound.
No kernel may reach another device: no remote copies, remote signals or barrier semaphores. Data moves between devices by JAX's collectives and lax.ppermute only.
A program may use at most 64 MiB of HBM per device.

```python
import math
import jax
import jax.numpy as jnp
from jax import lax

D = 4096
KS = 3
ORDER = 16
SEQ = 32768
N_CHAN = 32


def with_spikes(result, key, source, target, blocks, factor):
    owner, partner = [(jnp.arange(result.shape[dim]) // (result.shape[dim] // blocks)).reshape([-1 if axis == dim else 1 for axis in range(result.ndim)]) for dim in (source, target)]
    chosen = jax.random.permutation(key, blocks)[partner]
    strong = (owner == chosen) | (owner == (partner + blocks // 2) % blocks)
    return jnp.where(strong, factor * result, result)


def block_levels(stream_key, extent, cuts, low, top_value):
    level = 1.0
    for dim, shards_of in cuts:
        steps = jax.random.uniform(jax.random.fold_in(jax.random.fold_in(stream_key, 6), dim), (shards_of,), jnp.float32, low / len(cuts), top_value / len(cuts))
        level = level * jnp.repeat(jnp.exp(steps), extent[dim] // shards_of).reshape((-1,) + (1,) * (len(extent) - 1 - dim))
    return level


def normal_values(stream_key, extent, scale, reach, cuts=(), kind=jnp.bfloat16):
    values = jax.random.normal(stream_key, extent, jnp.float32) * scale
    if len(cuts) > 0:
        values = block_levels(stream_key, extent, cuts, -0.22, 0.18) * values
    return jnp.clip(values, min=-reach, max=reach).astype(kind)


def gaussian_with(stream_key, extent, scale, most, shards, heavy, dtype=jnp.bfloat16):
    entries = scale * jax.random.normal(stream_key, extent, jnp.float32)
    if shards:
        entries = entries * block_levels(stream_key, extent, shards, -0.22, 0.18)
    return jnp.clip(with_spikes(entries, jax.random.fold_in(stream_key, 3), *heavy), -most, most).astype(dtype)


def setup_inputs(seed: int = 0) -> dict:
    seeds = jax.random.split(jax.random.key(seed), 9)
    key_proj = normal_values(seeds[0], (SEQ, D), 1.0, 6.0, ((0, 32), (1, 32)))
    value_proj = normal_values(seeds[1], (SEQ, D), 1.0, 6.0, ((0, 32), (1, 32)))
    query_proj = normal_values(seeds[2], (SEQ, D), 1.0, 6.0, ((0, 32), (1, 32)))
    short_filter = normal_values(seeds[3], (3, KS, D), KS ** -0.5, 3.5, ((2, 32),))
    decay_rate = jnp.clip(jnp.exp(math.log(0.05) - 8.094623 * jax.random.uniform(seeds[4], (ORDER, D), jnp.float32) ** block_levels(seeds[4], (ORDER, D), ((1, 32),), -0.2, 0.2)), 1.52587890625e-05, 0.05)
    residue = normal_values(seeds[5], (ORDER, D), 0.004, 0.03, ((1, 32),), jnp.float32)
    skip_gain = jnp.clip(jax.random.uniform(seeds[6], (D,), jnp.float32, -1.0, 1.0) * block_levels(seeds[6], (D,), ((0, 32),), -0.4, 0.0), -1.0, 1.0)
    out_weight = gaussian_with(seeds[7], (D, D), D ** -0.5, 0.1875, ((0, 32),), (0, 1, 32, 2.75))
    return {"key_proj": key_proj, "value_proj": value_proj, "query_proj": query_proj, "short_filter": short_filter, "decay_rate": decay_rate, "residue": residue, "skip_gain": skip_gain, "out_weight": out_weight}


def short_conv(signal, filter_taps):
    tap_count = filter_taps.shape[0]
    length = signal.shape[0]
    padded = jnp.pad(signal, ((tap_count - 1, 0), (0, 0)))
    running = jnp.zeros(signal.shape, jnp.float32)
    for tap_index in range(tap_count):
        offset = tap_count - 1 - tap_index
        running = running + filter_taps[tap_index][None, :] * padded[offset:offset + length]
    return running


def modal_conv(signal, decay_rate, residue):
    channels, length = signal.shape
    tile_rows = 128
    blocks = length // tile_rows
    rates = decay_rate.T
    weights = residue.T
    position = jnp.arange(tile_rows).astype(jnp.float32)
    kernel = jnp.einsum('cm,cml->cl', weights, jnp.exp(-rates[:, :, None] * position[None, None, :]), precision=lax.Precision.HIGHEST)
    lag_index = jnp.arange(tile_rows)[:, None] - jnp.arange(tile_rows)[None, :]
    toeplitz = jnp.where(lag_index[None] >= 0, kernel[:, jnp.clip(lag_index, 0, tile_rows - 1)], jnp.float32(0.0))
    tiles = signal.reshape(channels, blocks, tile_rows)
    inside = jnp.einsum('cij,cnj->cni', toeplitz, tiles, precision=lax.Precision.HIGHEST)
    leaving = jnp.exp(-rates[:, :, None] * (tile_rows - position)[None, None, :])
    deposit = jnp.einsum('cmj,cnj->cnm', leaving, tiles, precision=lax.Precision.HIGHEST)
    factor = jnp.broadcast_to(jnp.exp(-rates * tile_rows)[:, None, :], deposit.shape)

    def combine(first, second):
        return (first[0] * second[0], first[1] * second[0] + second[1])

    _, ending = lax.associative_scan(combine, (factor, deposit), axis=1)
    starting = jnp.concatenate([jnp.zeros_like(ending[:, :1]), ending[:, :-1]], 1)
    arriving = weights[:, :, None] * jnp.exp(-rates[:, :, None] * position[None, None, :])
    carried = jnp.einsum('cnm,cmi->cni', starting, arriving, precision=lax.Precision.HIGHEST)
    return (inside + carried).reshape(channels, length), ending[:, -1]


def regroup(array_in):
    return array_in.reshape(array_in.shape[0], N_CHAN, -1).transpose(1, 0, 2)


def reference(key_proj, value_proj, query_proj, short_filter, decay_rate, residue, skip_gain, out_weight):
    filter_groups = short_filter.reshape(3, KS, N_CHAN, -1).transpose(2, 0, 1, 3)

    def per_group(inputs_group):
        key_group, value_group, query_group, filter_group, rate_group, residue_group, skip_group = inputs_group
        taps = filter_group.astype(jnp.float32)
        feat_query = short_conv(query_group.astype(jnp.float32), taps[0])
        feat_key = short_conv(key_group.astype(jnp.float32), taps[1])
        feat_value = short_conv(value_group.astype(jnp.float32), taps[2])
        product = (feat_key * feat_value).astype(jnp.bfloat16)
        signal = product.T.astype(jnp.float32)
        conv, _ = modal_conv(signal, rate_group, residue_group)
        long_out = (conv + skip_group[:, None] * signal).astype(jnp.bfloat16).T
        return (feat_query * long_out.astype(jnp.float32)).astype(jnp.bfloat16)

    grouped = lax.map(per_group, (regroup(key_proj), regroup(value_proj), regroup(query_proj), filter_groups, regroup(decay_rate), regroup(residue), skip_gain.reshape(N_CHAN, -1)))
    weight_groups = out_weight.reshape(N_CHAN, -1, D)

    def accumulate(running, operands):
        partial_sum = jnp.dot(operands[0], operands[1], preferred_element_type=jnp.float32).astype(jnp.bfloat16)
        return running + partial_sum.astype(jnp.float32), None

    summed, _ = lax.scan(accumulate, jnp.zeros((SEQ, D), jnp.float32), (grouped, weight_groups))
    return summed.astype(jnp.bfloat16)
```

```python
from functools import partial

import jax
import jax.numpy as jnp
from jax import lax
from jax.experimental import pallas as pl
from jax.experimental.pallas import tpu as pltpu
from jax.sharding import Mesh, PartitionSpec as P


CTX = ("w", "x", "core")
CHUNKS = 8


def features(padded, ref, tail, taps):
    rows = ref.shape[0]
    padded[6:8, :] = tail.astype(jnp.float32)
    padded[8:, :] = ref[...].astype(jnp.float32)
    total = taps[0:1, :] * padded[8 : 8 + rows, :]
    total = total + taps[1:2, :] * padded[7 : 7 + rows, :]
    return total + taps[2:3, :] * padded[6 : 6 + rows, :]


def first_pass(q, k, v, tail, taps, rates, featq, product, prefix, message, padded, signal):
    rows, chans = q.shape
    length = rows // CHUNKS
    modes = rates.shape[0]
    weights = taps[...].astype(jnp.float32)
    featq[...] = features(padded, q, tail[0], weights[0])
    last_query = padded[rows + 6 :, :]
    keyed = features(padded, k, tail[1], weights[1])
    last_key = padded[rows + 6 :, :]
    valued = features(padded, v, tail[2], weights[2])
    last_value = padded[rows + 6 :, :]
    edges = [keyed[0:2, :], valued[0:2, :], last_key, last_value, last_query]
    edges.append(jnp.zeros((6, chans), jnp.float32))
    prod = (keyed * valued).astype(jnp.bfloat16).astype(jnp.float32)
    product[...] = prod
    signal[...] = prod
    decay = [
        jnp.broadcast_to(jnp.exp(-rates[m : m + 1, :]), (CHUNKS, chans)) for m in range(modes)
    ]

    def step(t, held):
        row = signal[pl.ds(t, CHUNKS, stride=length), :]
        return tuple(decay[m] * held[m] + row for m in range(modes))

    zero = jnp.zeros((CHUNKS, chans), jnp.float32)
    held = lax.fori_loop(0, length, step, (zero,) * modes, unroll=4)
    index = lax.broadcasted_iota(jnp.int32, (CHUNKS, chans), 0)
    left = []
    for m in range(modes):
        rate = rates[m : m + 1, :]
        run = held[m]
        reach = 1
        while reach < CHUNKS:
            before = jnp.where(index >= reach, pltpu.roll(run, reach, 0), 0.0)
            run = run + jnp.exp(-rate * float(length * reach)) * before
            reach *= 2
        prefix[m] = jnp.where(index >= 1, pltpu.roll(run, 1, 0), 0.0)
        left.append(run[CHUNKS - 1 :, :])
    message[...] = jnp.concatenate(left + edges, axis=0)


def joined(rates, own, *rest, axis, span):
    *others, out, before = rest
    values = [own[...]] + [o[...] for o in others]
    modes = rates.shape[0]
    count = len(values)
    here = lax.axis_index(axis)
    decay = jnp.exp(-rates[...] * float(span))
    total = ahead = jnp.zeros(rates.shape, jnp.float32)
    ends = []
    for i in range(count):
        value = values[0]
        for d in range(1, count):
            value = jnp.where(lax.rem(here - d + count, count) == i, values[d], value)
        ends.append(value)
        ahead = jnp.where(i < here, decay * ahead + value[0:modes, :], ahead)
        total = decay * total + value[0:modes, :]
    row = lax.broadcasted_iota(jnp.int32, own.shape, 0)
    edges = jnp.where(row < modes + 4, ends[0], ends[-1])
    out[...] = jnp.concatenate([total, edges[modes:, :]], axis=0)
    before[...] = ahead


def edge_change(message, before, taps, modes):
    def pair(head, tail, weights):
        old0 = message[modes + head : modes + head + 1, :]
        old1 = message[modes + head + 1 : modes + head + 2, :]
        back2 = before[modes + tail : modes + tail + 1, :]
        back1 = before[modes + tail + 1 : modes + tail + 2, :]
        new0 = (old0 + weights[1:2, :] * back1) + weights[2:3, :] * back2
        return old0, old1, new0, old1 + weights[2:3, :] * back1

    def rounded(value):
        return value.astype(jnp.bfloat16).astype(jnp.float32)

    k0, k1, kn0, kn1 = pair(0, 4, taps[1])
    v0, v1, vn0, vn1 = pair(2, 6, taps[2])
    return rounded(kn0 * vn0) - rounded(k0 * v0), rounded(kn1 * vn1) - rounded(k1 * v1)


def second_pass(
    featq, product, prefix, low, mid, own, back1, back2, back3,
    taps, rates, residue, gain, gated, signal, mixed,
):
    rows, chans = product.shape
    length = rows // CHUNKS
    modes = rates.shape[0]
    ncore, nx = lax.axis_size("core"), lax.axis_size("x")
    run = rows * ncore * nx
    core, x = lax.axis_index("core"), lax.axis_index("x")
    rate = rates[...]
    weights = taps[...].astype(jnp.float32)

    def power(tokens):
        return jnp.exp(-rate * tokens)

    chain = [own[...], back1[...], back2[...], back3[...], jnp.zeros(own.shape, jnp.float32)]
    start = jnp.zeros((modes, chans), jnp.float32)
    whole = power(float(run))
    for d in (3, 2, 1):
        first, second = edge_change(chain[d], chain[d + 1], weights, modes)
        total = chain[d][0:modes, :] + power(run - 1.0) * first + power(run - 2.0) * second
        start = whole * start + total
    first, second = edge_change(chain[0], chain[1], weights, modes)
    lost = jnp.exp(rate) * first + jnp.exp(2.0 * rate) * second
    ahead = (x * ncore + core).astype(jnp.float32) * float(rows)
    leads = ahead < 1.0
    back_core = power(core.astype(jnp.float32) * float(rows))
    carried = low[...] + back_core * mid[...] + power(ahead) * (start + jnp.where(leads, 0.0, lost))
    lost = jnp.where(leads, lost, 0.0)

    wide = (CHUNKS, chans)
    row = lax.broadcasted_iota(jnp.int32, wide, 0)
    index = row.astype(jnp.float32)
    dp0, dp1 = jnp.where(leads, first, 0.0), jnp.where(leads, second, 0.0)
    signal[...] = product[...]
    signal[0:CHUNKS, :] = product[0:CHUNKS, :] + jnp.where(
        row == 0, dp0, jnp.where(row == 1, dp1, 0.0)
    )
    held = []
    decay = []
    weight = []
    for m in range(modes):
        one = rate[m : m + 1, :]
        decay.append(jnp.broadcast_to(jnp.exp(-one), wide))
        weight.append(jnp.broadcast_to(residue[m : m + 1, :], wide))
        reach = jnp.exp(-one * (index * float(length)))
        before = carried[m : m + 1, :] + jnp.where(row >= 1, lost[m : m + 1, :], 0.0)
        held.append(prefix[m] + reach * before)

    def step(t, held):
        now = signal[pl.ds(t, CHUNKS, stride=length), :]
        held = tuple(decay[m] * held[m] + now for m in range(modes))
        terms = [weight[m] * held[m] for m in range(modes)]
        while len(terms) > 1:
            terms = [terms[i] + terms[i + 1] for i in range(0, len(terms), 2)]
        mixed[pl.ds(t, CHUNKS, stride=length), :] = terms[0]
        return held

    lax.fori_loop(0, length, step, tuple(held), unroll=2)
    long_out = (mixed[...] + gain[...] * signal[...]).astype(jnp.bfloat16).astype(jnp.float32)
    gated[...] = (featq[...] * long_out).astype(jnp.bfloat16)
    last2 = back1[modes + 8 : modes + 9, :]
    last1 = back1[modes + 9 : modes + 10, :]
    top = lax.broadcasted_iota(jnp.int32, (16, chans), 0)
    dq0 = jnp.where(leads, weights[0][1:2, :] * last1 + weights[0][2:3, :] * last2, 0.0)
    dq1 = jnp.where(leads, weights[0][2:3, :] * last1, 0.0)
    query = featq[0:16, :] + jnp.where(top == 0, dq0, jnp.where(top == 1, dq1, 0.0))
    gated[0:16, :] = (query * long_out[0:16, :]).astype(jnp.bfloat16)


def project(gathered, weights, shares):
    ny, nb = gathered.shape[:2]
    ncore, nx = weights.shape[:2]
    left = jnp.concatenate(
        [gathered[i, j] for i in range(ny) for j in range(nb)], axis=1
    )
    width = shares.shape[2]
    for n in range(0, shares.shape[0], 2):
        cols = slice(n * width, (n + 2) * width)
        right = jnp.concatenate(
            [
                weights[core, x, i, j, :, cols]
                for i in range(ny)
                for j in range(nb)
                for x in range(nx)
                for core in range(ncore)
            ],
            axis=0,
        )
        both = jnp.dot(left, right, preferred_element_type=jnp.float32).astype(shares.dtype)
        shares[n] = both[:, :width]
        shares[n + 1] = both[:, width:]


def moved(value, axis, pairs):
    return lax.ppermute(value, axis, pairs)


def everyone(value, axis):
    count = lax.axis_size(axis)
    return lax.all_to_all(
        jnp.broadcast_to(value[None], (count,) + value.shape), axis, 0, 0, tiled=True
    )


def own_weights(out_weight):
    ny, nb = lax.axis_size("y"), lax.axis_size("zb")
    ncore = lax.axis_size("core")
    share = out_weight.shape[0] // (lax.axis_size("x") * ncore)
    first = (lax.axis_index("x") * ncore + lax.axis_index("core")) * share
    rows = lax.dynamic_slice_in_dim(out_weight, first, share, 0)
    blocks = rows.reshape(share, ny, -1).transpose(1, 0, 2)
    blocks = jnp.broadcast_to(blocks[:, None], (ny, nb) + blocks.shape[1:])
    blocks = blocks.reshape((ny * nb,) + blocks.shape[2:])
    got = lax.all_to_all(blocks, ("y", "zb"), 0, 0, tiled=True)
    return got.reshape((ny, nb) + got.shape[1:])


def layer(
    key_proj, value_proj, query_proj, short_filter, decay_rate, residue, skip_gain, out_weight
):
    rows, chans = key_proj.shape
    modes = decay_rate.shape[0]
    na, nb = lax.axis_size("za"), lax.axis_size("zb")
    ncore, nx, nw = (lax.axis_size(a) for a in ("core", "x", "w"))
    f32 = jnp.float32
    weights = own_weights(out_weight)
    tails = jnp.stack([query_proj[rows - 2 :], key_proj[rows - 2 :], value_proj[rows - 2 :]], 0)
    near = [(i, i + 1) for i in range(nw * nx * ncore - 1) if (i + 1) % (nx * ncore) > 0]
    tails = moved(tails, CTX, near)
    featq, product, prefix, message = pl.pallas_call(
        first_pass,
        out_shape=(
            jax.ShapeDtypeStruct((rows, chans), f32),
            jax.ShapeDtypeStruct((rows, chans), f32),
            jax.ShapeDtypeStruct((modes, CHUNKS, chans), f32),
            jax.ShapeDtypeStruct((modes + 16, chans), f32),
        ),
        scratch_shapes=[pltpu.VMEM((rows + 8, chans), f32), pltpu.VMEM((rows, chans), f32)],
        name="first_pass",
    )(query_proj, key_proj, value_proj, tails, short_filter, decay_rate)

    def join(value, axis, span):
        count = lax.axis_size(axis)
        rest = [
            moved(value, axis, [(i, (i + d) % count) for i in range(count)])
            for d in range(1, count)
        ]
        return pl.pallas_call(
            partial(joined, axis=axis, span=span),
            out_shape=(
                jax.ShapeDtypeStruct((modes + 16, chans), f32),
                jax.ShapeDtypeStruct((modes, chans), f32),
            ),
        )(decay_rate, value, *rest)

    message, low = join(message, "core", rows)
    own, mid = join(message, "x", rows * ncore)
    weights, own = lax.optimization_barrier((weights, own))
    weights = everyone(weights, "x")
    back = {}
    for d in (2, 1, 3):
        back[d] = moved(own, "w", [(i, i + d) for i in range(nw - d)])
    gated = pl.pallas_call(
        second_pass,
        out_shape=jax.ShapeDtypeStruct((rows, chans), jnp.bfloat16),
        scratch_shapes=[pltpu.VMEM((rows, chans), f32), pltpu.VMEM((rows, chans), f32)],
        name="second_pass",
    )(
        featq, product, prefix, low, mid, own, back[1], back[2], back[3],
        short_filter, decay_rate, residue, skip_gain[None],
    )
    weights = everyone(weights, "core")
    quarter = rows // nb
    mine = lax.all_to_all(gated.reshape(nb, quarter, chans), "zb", 0, 0, tiled=True)
    gathered = everyone(mine, "y")
    shares = pl.pallas_call(
        project,
        out_shape=jax.ShapeDtypeStruct((na * nb, quarter, chans), jnp.bfloat16),
        name="project",
    )(gathered, weights)
    parts = lax.all_to_all(shares, ("za", "zb"), 0, 0, tiled=True)
    total = parts.reshape(na, rows, chans).astype(f32).sum(0)
    return total.astype(jnp.bfloat16)


def solution(mesh):
    fine = Mesh(mesh.devices.reshape(4, 2, 4, 4, 4, 2), ("y", "za", "zb") + CTX)
    chan = ("y", "za", "zb")
    placed = (
        P(CTX, chan),
        P(CTX, chan),
        P(CTX, chan),
        P(None, None, chan),
        P(None, chan),
        P(None, chan),
        P(chan),
        P(chan, None),
    )
    return jax.shard_map(layer, mesh=fine, in_specs=placed, out_specs=P(CTX, chan), check_vma=False)
```

```python
from functools import partial

import jax
import jax.numpy as jnp
from jax import lax
from jax.experimental import pallas as pl
from jax.experimental.pallas import tpu as pltpu
from jax.sharding import Mesh, PartitionSpec as P


CTX = ("w", "xa", "xb", "core")
X = ("xa", "xb")
CHUNKS = 8


def features(padded, ref, tail, taps):
    rows = ref.shape[0]
    padded[6:8, :] = tail.astype(jnp.float32)
    padded[8:, :] = ref[...].astype(jnp.float32)
    total = taps[0:1, :] * padded[8 : 8 + rows, :]
    total = total + taps[1:2, :] * padded[7 : 7 + rows, :]
    return total + taps[2:3, :] * padded[6 : 6 + rows, :]


def first_pass(q, k, v, tail, taps, rates, featq, product, prefix, message, padded, signal):
    rows, chans = q.shape
    length = rows // CHUNKS
    modes = rates.shape[0]
    weights = taps[...].astype(jnp.float32)
    featq[...] = features(padded, q, tail[0], weights[0])
    last_query = padded[rows + 6 :, :]
    keyed = features(padded, k, tail[1], weights[1])
    last_key = padded[rows + 6 :, :]
    valued = features(padded, v, tail[2], weights[2])
    last_value = padded[rows + 6 :, :]
    edges = [keyed[0:2, :], valued[0:2, :], last_key, last_value, last_query]
    edges.append(jnp.zeros((6, chans), jnp.float32))
    prod = (keyed * valued).astype(jnp.bfloat16).astype(jnp.float32)
    product[...] = prod
    signal[...] = prod
    decay = [
        jnp.broadcast_to(jnp.exp(-rates[m : m + 1, :]), (CHUNKS, chans)) for m in range(modes)
    ]

    def step(t, held):
        row = signal[pl.ds(t, CHUNKS, stride=length), :]
        return tuple(decay[m] * held[m] + row for m in range(modes))

    zero = jnp.zeros((CHUNKS, chans), jnp.float32)
    held = lax.fori_loop(0, length, step, (zero,) * modes, unroll=4)
    index = lax.broadcasted_iota(jnp.int32, (CHUNKS, chans), 0)
    left = []
    for m in range(modes):
        rate = rates[m : m + 1, :]
        run = held[m]
        reach = 1
        while reach < CHUNKS:
            before = jnp.where(index >= reach, pltpu.roll(run, reach, 0), 0.0)
            run = run + jnp.exp(-rate * float(length * reach)) * before
            reach *= 2
        prefix[m] = jnp.where(index >= 1, pltpu.roll(run, 1, 0), 0.0)
        left.append(run[CHUNKS - 1 :, :])
    message[...] = jnp.concatenate(left + edges, axis=0)


def joined(rates, own, *rest, axis, span):
    *others, out, before = rest
    values = [own[...]] + [o[...] for o in others]
    modes = rates.shape[0]
    count = len(values)
    here = lax.axis_index(axis)
    decay = jnp.exp(-rates[...] * float(span))
    total = ahead = jnp.zeros(rates.shape, jnp.float32)
    ends = []
    for i in range(count):
        value = values[0]
        for d in range(1, count):
            value = jnp.where(lax.rem(here - d + count, count) == i, values[d], value)
        ends.append(value)
        ahead = jnp.where(i < here, decay * ahead + value[0:modes, :], ahead)
        total = decay * total + value[0:modes, :]
    row = lax.broadcasted_iota(jnp.int32, own.shape, 0)
    edges = jnp.where(row < modes + 4, ends[0], ends[-1])
    out[...] = jnp.concatenate([total, edges[modes:, :]], axis=0)
    before[...] = ahead


def edge_change(message, before, taps, modes):
    def pair(head, tail, weights):
        old0 = message[modes + head : modes + head + 1, :]
        old1 = message[modes + head + 1 : modes + head + 2, :]
        back2 = before[modes + tail : modes + tail + 1, :]
        back1 = before[modes + tail + 1 : modes + tail + 2, :]
        new0 = (old0 + weights[1:2, :] * back1) + weights[2:3, :] * back2
        return old0, old1, new0, old1 + weights[2:3, :] * back1

    def rounded(value):
        return value.astype(jnp.bfloat16).astype(jnp.float32)

    k0, k1, kn0, kn1 = pair(0, 4, taps[1])
    v0, v1, vn0, vn1 = pair(2, 6, taps[2])
    return rounded(kn0 * vn0) - rounded(k0 * v0), rounded(kn1 * vn1) - rounded(k1 * v1)


def second_pass(
    featq, product, prefix, low, mid, high, own, back1, back2, back3,
    taps, rates, residue, gain, gated, signal, mixed,
):
    rows, chans = product.shape
    length = rows // CHUNKS
    modes = rates.shape[0]
    core, xb, xa = (lax.axis_index(a) for a in ("core", "xb", "xa"))
    two = rows * lax.axis_size("core")
    four = two * lax.axis_size("xb")
    run = four * lax.axis_size("xa")
    rate = rates[...]
    weights = taps[...].astype(jnp.float32)

    def power(tokens):
        return jnp.exp(-rate * tokens)

    chain = [own[...], back1[...], back2[...], back3[...], jnp.zeros(own.shape, jnp.float32)]
    start = jnp.zeros((modes, chans), jnp.float32)
    whole = power(float(run))
    for d in (3, 2, 1):
        first, second = edge_change(chain[d], chain[d + 1], weights, modes)
        total = chain[d][0:modes, :] + power(run - 1.0) * first + power(run - 2.0) * second
        start = whole * start + total
    first, second = edge_change(chain[0], chain[1], weights, modes)
    lost = jnp.exp(rate) * first + jnp.exp(2.0 * rate) * second
    ahead = (core * rows + xb * two + xa * four).astype(jnp.float32)
    leads = ahead < 1.0
    carried = start + jnp.where(leads, 0.0, lost)
    for part, place, span in ((high, xa, four), (mid, xb, two), (low, core, rows)):
        carried = part[...] + power(place.astype(jnp.float32) * float(span)) * carried
    lost = jnp.where(leads, lost, 0.0)

    wide = (CHUNKS, chans)
    row = lax.broadcasted_iota(jnp.int32, wide, 0)
    index = row.astype(jnp.float32)
    dp0, dp1 = jnp.where(leads, first, 0.0), jnp.where(leads, second, 0.0)
    signal[...] = product[...]
    signal[0:CHUNKS, :] = product[0:CHUNKS, :] + jnp.where(
        row == 0, dp0, jnp.where(row == 1, dp1, 0.0)
    )
    held = []
    decay = []
    weight = []
    for m in range(modes):
        one = rate[m : m + 1, :]
        decay.append(jnp.broadcast_to(jnp.exp(-one), wide))
        weight.append(jnp.broadcast_to(residue[m : m + 1, :], wide))
        reach = jnp.exp(-one * (index * float(length)))
        before = carried[m : m + 1, :] + jnp.where(row >= 1, lost[m : m + 1, :], 0.0)
        held.append(prefix[m] + reach * before)

    def step(t, held):
        now = signal[pl.ds(t, CHUNKS, stride=length), :]
        held = tuple(decay[m] * held[m] + now for m in range(modes))
        terms = [weight[m] * held[m] for m in range(modes)]
        while len(terms) > 1:
            terms = [terms[i] + terms[i + 1] for i in range(0, len(terms), 2)]
        mixed[pl.ds(t, CHUNKS, stride=length), :] = terms[0]
        return held

    lax.fori_loop(0, length, step, tuple(held), unroll=2)
    long_out = (mixed[...] + gain[...] * signal[...]).astype(jnp.bfloat16).astype(jnp.float32)
    gated[...] = (featq[...] * long_out).astype(jnp.bfloat16)
    last2 = back1[modes + 8 : modes + 9, :]
    last1 = back1[modes + 9 : modes + 10, :]
    top = lax.broadcasted_iota(jnp.int32, (16, chans), 0)
    dq0 = jnp.where(leads, weights[0][1:2, :] * last1 + weights[0][2:3, :] * last2, 0.0)
    dq1 = jnp.where(leads, weights[0][2:3, :] * last1, 0.0)
    query = featq[0:16, :] + jnp.where(top == 0, dq0, jnp.where(top == 1, dq1, 0.0))
    gated[0:16, :] = (query * long_out[0:16, :]).astype(jnp.bfloat16)


def project(gathered, mine, other, shares):
    ny, nb = gathered.shape[:2]
    nx = mine.shape[0]
    core = lax.axis_index("core")
    width = shares.shape[2]

    def run(halves):
        left = jnp.concatenate([gathered[i, j] for i in range(ny) for j in range(nb)], axis=1)
        for n in range(0, shares.shape[0], 2):
            cols = slice(n * width, (n + 2) * width)
            right = jnp.concatenate(
                [
                    half[x, i, j, :, cols]
                    for i in range(ny)
                    for j in range(nb)
                    for x in range(nx)
                    for half in halves
                ],
                axis=0,
            )
            both = jnp.dot(left, right, preferred_element_type=jnp.float32).astype(shares.dtype)
            shares[n] = both[:, :width]
            shares[n + 1] = both[:, width:]

    @pl.when(core == 0)
    def _():
        run((mine, other))

    @pl.when(core == 1)
    def _():
        run((other, mine))


def moved(value, axis, pairs):
    return lax.ppermute(value, axis, pairs)


def near_vmem(value):
    return pltpu.with_memory_space_constraint(value, pltpu.VMEM)


def everyone(value, axis):
    count = lax.axis_size(axis)
    return lax.all_to_all(
        jnp.broadcast_to(value[None], (count,) + value.shape), axis, 0, 0, tiled=True
    )


def own_weights(out_weight):
    ny, nb = lax.axis_size("y"), lax.axis_size("zb")
    ncore = lax.axis_size("core")
    share = out_weight.shape[0] // (lax.axis_size(X) * ncore)
    first = (lax.axis_index(X) * ncore + lax.axis_index("core")) * share
    rows = lax.dynamic_slice_in_dim(out_weight, first, share, 0)
    blocks = rows.reshape(share, ny, -1).transpose(1, 0, 2)
    blocks = jnp.broadcast_to(blocks[:, None], (ny, nb) + blocks.shape[1:])
    blocks = blocks.reshape((ny * nb,) + blocks.shape[2:])
    got = lax.all_to_all(blocks, ("y", "zb"), 0, 0, tiled=True)
    return got.reshape((ny, nb) + got.shape[1:])


def layer(
    key_proj, value_proj, query_proj, short_filter, decay_rate, residue, skip_gain, out_weight
):
    rows, chans = key_proj.shape
    modes = decay_rate.shape[0]
    na, nb = lax.axis_size("za"), lax.axis_size("zb")
    ncore, nx, nw = (lax.axis_size(a) for a in ("core", X, "w"))
    f32 = jnp.float32
    weights = own_weights(out_weight)
    tails = jnp.stack([query_proj[rows - 2 :], key_proj[rows - 2 :], value_proj[rows - 2 :]], 0)
    near = [(i, i + 1) for i in range(nw * nx * ncore - 1) if (i + 1) % (nx * ncore) > 0]
    tails = moved(tails, CTX, near)
    featq, product, prefix, message = pl.pallas_call(
        first_pass,
        out_shape=(
            jax.ShapeDtypeStruct((rows, chans), f32),
            jax.ShapeDtypeStruct((rows, chans), f32),
            jax.ShapeDtypeStruct((modes, CHUNKS, chans), f32),
            pltpu.VMEM((modes + 16, chans), f32),
        ),
        in_specs=[pl.BlockSpec(memory_space=pltpu.VMEM)] * 6,
        out_specs=(pl.BlockSpec(memory_space=pltpu.VMEM),) * 4,
        scratch_shapes=[pltpu.VMEM((rows + 8, chans), f32), pltpu.VMEM((rows, chans), f32)],
        name="first_pass",
    )(query_proj, key_proj, value_proj, near_vmem(tails), short_filter, decay_rate)

    def join(value, axis, span):
        count = lax.axis_size(axis)
        rest = [
            moved(value, axis, [(i, (i + d) % count) for i in range(count)])
            for d in range(1, count)
        ]
        return pl.pallas_call(
            partial(joined, axis=axis, span=span),
            out_shape=(
                pltpu.VMEM((modes + 16, chans), f32),
                pltpu.VMEM((modes, chans), f32),
            ),
            in_specs=[pl.BlockSpec(memory_space=pltpu.VMEM)] * (count + 1),
            out_specs=(pl.BlockSpec(memory_space=pltpu.VMEM),) * 2,
        )(decay_rate, near_vmem(value), *[near_vmem(r) for r in rest])

    message, low = join(message, "core", rows)
    message, mid = join(message, "xb", rows * ncore)
    own, high = join(message, "xa", rows * ncore * lax.axis_size("xb"))
    back = {}
    back[1] = moved(own, "w", [(i, i + 1) for i in range(nw - 1)])
    back[3] = moved(own, "w", [(0, nw - 1)])
    weights = everyone(weights, X)
    held = jnp.where(lax.axis_index("w") == nw - 1, back[3], back[1])
    back[2] = moved(held, "w", [(nw - 2, nw - 1), (nw - 1, nw - 2)])
    gated = pl.pallas_call(
        second_pass,
        out_shape=jax.ShapeDtypeStruct((rows, chans), jnp.bfloat16),
        scratch_shapes=[pltpu.VMEM((rows, chans), f32), pltpu.VMEM((rows, chans), f32)],
        in_specs=[pl.BlockSpec(memory_space=pltpu.VMEM)] * 14,
        out_specs=pl.BlockSpec(memory_space=pltpu.VMEM),
        name="second_pass",
    )(
        featq, product, prefix, *[near_vmem(v) for v in (low, mid, high, own)],
        *[near_vmem(back[d]) for d in (1, 2, 3)],
        short_filter, decay_rate, residue, skip_gain[None],
    )
    other = moved(weights, "core", [(0, 1), (1, 0)])
    quarter = rows // nb
    mine = lax.all_to_all(gated.reshape(nb, quarter, chans), "zb", 0, 0, tiled=True)
    gathered = everyone(mine, "y")
    shares = pl.pallas_call(
        project,
        out_shape=jax.ShapeDtypeStruct((na * nb, quarter, chans), jnp.bfloat16),
        name="project",
    )(gathered, weights, other)
    parts = lax.all_to_all(shares, ("za", "zb"), 0, 0, tiled=True)
    total = parts.reshape(na, rows, chans).astype(f32).sum(0)
    return total.astype(jnp.bfloat16)


def solution(mesh):
    fine = Mesh(mesh.devices.reshape(4, 2, 4, 4, 2, 2, 2), ("y", "za", "zb") + CTX)
    chan = ("y", "za", "zb")
    placed = (
        P(CTX, chan),
        P(CTX, chan),
        P(CTX, chan),
        P(None, None, chan),
        P(None, chan),
        P(None, chan),
        P(chan),
        P(chan, None),
    )
    return jax.shard_map(layer, mesh=fine, in_specs=placed, out_specs=P(CTX, chan), check_vma=False)
```

```python
from functools import partial

import jax
import jax.numpy as jnp
from jax import lax
from jax.experimental import pallas as pl
from jax.experimental.pallas import tpu as pltpu
from jax.sharding import Mesh, PartitionSpec as P


CTX = ("w", "xa", "xb", "core")
X = ("xa", "xb")
CHUNKS = 8


def features(padded, ref, taps):
    rows = ref.shape[0]
    padded[0:8, :] = jnp.zeros((8, ref.shape[1]), jnp.float32)
    padded[8:, :] = ref[...].astype(jnp.float32)
    total = taps[0:1, :] * padded[8 : 8 + rows, :]
    total = total + taps[1:2, :] * padded[7 : 7 + rows, :]
    return total + taps[2:3, :] * padded[6 : 6 + rows, :]


def first_pass(q, k, v, taps, rates, featq, product, prefix, message, padded, signal):
    rows, chans = q.shape
    length = rows // CHUNKS
    modes = rates.shape[0]
    weights = taps[...].astype(jnp.float32)
    featq[...] = features(padded, q, weights[0])
    last_query = padded[rows + 6 :, :]
    keyed = features(padded, k, weights[1])
    last_key = padded[rows + 6 :, :]
    valued = features(padded, v, weights[2])
    last_value = padded[rows + 6 :, :]
    edges = [keyed[0:2, :], valued[0:2, :], last_key, last_value, last_query]
    edges.append(jnp.zeros((6, chans), jnp.float32))
    prod = (keyed * valued).astype(jnp.bfloat16).astype(jnp.float32)
    product[...] = prod
    signal[...] = prod
    decay = [
        jnp.broadcast_to(jnp.exp(-rates[m : m + 1, :]), (CHUNKS, chans)) for m in range(modes)
    ]

    def step(t, held):
        row = signal[pl.ds(t, CHUNKS, stride=length), :]
        return tuple(decay[m] * held[m] + row for m in range(modes))

    zero = jnp.zeros((CHUNKS, chans), jnp.float32)
    held = lax.fori_loop(0, length, step, (zero,) * modes, unroll=4)
    index = lax.broadcasted_iota(jnp.int32, (CHUNKS, chans), 0)
    left = []
    for m in range(modes):
        rate = rates[m : m + 1, :]
        run = held[m]
        reach = 1
        while reach < CHUNKS:
            before = jnp.where(index >= reach, pltpu.roll(run, reach, 0), 0.0)
            run = run + jnp.exp(-rate * float(length * reach)) * before
            reach *= 2
        prefix[m] = jnp.where(index >= 1, pltpu.roll(run, 1, 0), 0.0)
        left.append(run[CHUNKS - 1 :, :])
    message[...] = jnp.concatenate(left + edges, axis=0)


def joined(rates, taps, own, other, out, before, fix, *, axis, lower, span):
    modes = rates.shape[0]
    rate = rates[...]
    right_side = lax.axis_index(axis) == 1
    left = jnp.where(right_side, other[...], own[...])
    right = jnp.where(right_side, own[...], other[...])
    first, second = edge_change(right, left, taps[...].astype(jnp.float32), modes)
    total = jnp.exp(-rate * float(span)) * left[0:modes, :] + right[0:modes, :]
    total = total + jnp.exp(-rate * (span - 1.0)) * first
    total = total + jnp.exp(-rate * (span - 2.0)) * second
    row = lax.broadcasted_iota(jnp.int32, left.shape, 0)
    edges = jnp.where(row < modes + 4, left, right)
    out[...] = jnp.concatenate([total, edges[modes:, :]], axis=0)
    inside = sum((lax.axis_index(a) for a in lower), jnp.int32(0))
    lost = jnp.exp(rate) * first + jnp.exp(2.0 * rate) * second
    lost = jnp.where(inside > 0, lost, 0.0)
    before[...] = jnp.where(right_side, left[0:modes, :] + lost, 0.0)
    rows = [first, second, left[modes + 8 : modes + 10, :]]
    rows.append(jnp.zeros((4,) + first.shape[1:], jnp.float32))
    leads = jnp.logical_and(right_side, inside == 0)
    fix[...] = jnp.where(leads, jnp.concatenate(rows, axis=0), 0.0)


def edge_change(message, before, taps, modes):
    def pair(head, tail, weights):
        old0 = message[modes + head : modes + head + 1, :]
        old1 = message[modes + head + 1 : modes + head + 2, :]
        back2 = before[modes + tail : modes + tail + 1, :]
        back1 = before[modes + tail + 1 : modes + tail + 2, :]
        new0 = (old0 + weights[1:2, :] * back1) + weights[2:3, :] * back2
        return old0, old1, new0, old1 + weights[2:3, :] * back1

    def rounded(value):
        return value.astype(jnp.bfloat16).astype(jnp.float32)

    k0, k1, kn0, kn1 = pair(0, 4, taps[1])
    v0, v1, vn0, vn1 = pair(2, 6, taps[2])
    return rounded(kn0 * vn0) - rounded(k0 * v0), rounded(kn1 * vn1) - rounded(k1 * v1)


def second_pass(
    featq, product, prefix, low, mid, high, fix_low, fix_mid, fix_high,
    own, back1, back2, back3,
    taps, rates, residue, gain, gated, signal, mixed,
):
    rows, chans = product.shape
    length = rows // CHUNKS
    modes = rates.shape[0]
    core, xb, xa = (lax.axis_index(a) for a in ("core", "xb", "xa"))
    two = rows * lax.axis_size("core")
    four = two * lax.axis_size("xb")
    run = four * lax.axis_size("xa")
    rate = rates[...]
    weights = taps[...].astype(jnp.float32)

    def power(tokens):
        return jnp.exp(-rate * tokens)

    chain = [own[...], back1[...], back2[...], back3[...], jnp.zeros(own.shape, jnp.float32)]
    start = jnp.zeros((modes, chans), jnp.float32)
    whole = power(float(run))
    for d in (3, 2, 1):
        first, second = edge_change(chain[d], chain[d + 1], weights, modes)
        total = chain[d][0:modes, :] + power(run - 1.0) * first + power(run - 2.0) * second
        start = whole * start + total
    first, second = edge_change(chain[0], chain[1], weights, modes)
    lost = jnp.exp(rate) * first + jnp.exp(2.0 * rate) * second
    ahead = (core * rows + xb * two + xa * four).astype(jnp.float32)
    leads = ahead < 1.0
    carried = start + jnp.where(leads, 0.0, lost)
    for part, place, span in ((high, xa, four), (mid, xb, two), (low, core, rows)):
        carried = part[...] + power(place.astype(jnp.float32) * float(span)) * carried
    far = jnp.concatenate([first, second, back1[modes + 8 : modes + 10, :]], axis=0)
    fix = fix_low[...] + fix_mid[...] + fix_high[...]
    fix = fix[0:4, :] + jnp.where(leads, far, 0.0)
    dp0, dp1, last2, last1 = (fix[i : i + 1, :] for i in range(4))
    lost = jnp.exp(rate) * dp0 + jnp.exp(2.0 * rate) * dp1

    wide = (CHUNKS, chans)
    row = lax.broadcasted_iota(jnp.int32, wide, 0)
    index = row.astype(jnp.float32)
    signal[...] = product[...]
    signal[0:CHUNKS, :] = product[0:CHUNKS, :] + jnp.where(
        row == 0, dp0, jnp.where(row == 1, dp1, 0.0)
    )
    held = []
    decay = []
    weight = []
    for m in range(modes):
        one = rate[m : m + 1, :]
        decay.append(jnp.broadcast_to(jnp.exp(-one), wide))
        weight.append(jnp.broadcast_to(residue[m : m + 1, :], wide))
        reach = jnp.exp(-one * (index * float(length)))
        before = carried[m : m + 1, :] + jnp.where(row >= 1, lost[m : m + 1, :], 0.0)
        held.append(prefix[m] + reach * before)

    def step(t, held):
        now = signal[pl.ds(t, CHUNKS, stride=length), :]
        held = tuple(decay[m] * held[m] + now for m in range(modes))
        terms = [weight[m] * held[m] for m in range(modes)]
        while len(terms) > 1:
            terms = [terms[i] + terms[i + 1] for i in range(0, len(terms), 2)]
        mixed[pl.ds(t, CHUNKS, stride=length), :] = terms[0]
        return held

    lax.fori_loop(0, length, step, tuple(held), unroll=2)
    long_out = (mixed[...] + gain[...] * signal[...]).astype(jnp.bfloat16).astype(jnp.float32)
    gated[...] = (featq[...] * long_out).astype(jnp.bfloat16)
    top = lax.broadcasted_iota(jnp.int32, (16, chans), 0)
    dq0 = weights[0][1:2, :] * last1 + weights[0][2:3, :] * last2
    dq1 = weights[0][2:3, :] * last1
    query = featq[0:16, :] + jnp.where(top == 0, dq0, jnp.where(top == 1, dq1, 0.0))
    gated[0:16, :] = (query * long_out[0:16, :]).astype(jnp.bfloat16)


def project(gathered, mine, other, shares, buffer, sems):
    ny, nb = gathered.shape[:2]
    nx = mine.shape[0]
    core = lax.axis_index("core")
    here = lax.axis_index("xa") * lax.axis_size("xb") + lax.axis_index("xb")
    width = shares.shape[2]
    moves = []
    for d in range(nx):
        x = lax.rem(here - d + nx, nx)
        moves.append(pltpu.make_async_copy(mine.at[d], buffer.at[x, core], sems.at[2 * d]))
        moves.append(
            pltpu.make_async_copy(other.at[d], buffer.at[x, 1 - core], sems.at[2 * d + 1])
        )
    for move in moves:
        move.start()
    left = jnp.concatenate([gathered[i, j] for i in range(ny) for j in range(nb)], axis=1)
    for move in moves:
        move.wait()
    for n in range(0, shares.shape[0], 2):
        cols = slice(n * width, (n + 2) * width)
        right = jnp.concatenate(
            [
                buffer[x, c, i, j, :, cols]
                for i in range(ny)
                for j in range(nb)
                for x in range(nx)
                for c in range(2)
            ],
            axis=0,
        )
        both = jnp.dot(left, right, preferred_element_type=jnp.float32).astype(shares.dtype)
        shares[n] = both[:, :width]
        shares[n + 1] = both[:, width:]


def moved(value, axis, pairs):
    return lax.ppermute(value, axis, pairs)


def near_vmem(value):
    return pltpu.with_memory_space_constraint(value, pltpu.VMEM)


def own_weights(out_weight):
    ny, nb = lax.axis_size("y"), lax.axis_size("zb")
    ncore = lax.axis_size("core")
    share = out_weight.shape[0] // (lax.axis_size(X) * ncore)
    first = (lax.axis_index(X) * ncore + lax.axis_index("core")) * share
    rows = lax.dynamic_slice_in_dim(out_weight, first, share, 0)
    blocks = rows.reshape(share, ny, -1).transpose(1, 0, 2)
    blocks = jnp.broadcast_to(blocks[:, None], (ny, nb) + blocks.shape[1:])
    blocks = blocks.reshape((ny * nb,) + blocks.shape[2:])
    got = lax.all_to_all(blocks, ("y", "zb"), 0, 0, tiled=True)
    return got.reshape((ny, nb) + got.shape[1:])


def layer(
    key_proj, value_proj, query_proj, short_filter, decay_rate, residue, skip_gain, out_weight
):
    rows, chans = key_proj.shape
    modes = decay_rate.shape[0]
    na, nb = lax.axis_size("za"), lax.axis_size("zb")
    ncore, nw = lax.axis_size("core"), lax.axis_size("w")
    f32 = jnp.float32
    weights = own_weights(out_weight)
    featq, product, prefix, message = pl.pallas_call(
        first_pass,
        out_shape=(
            jax.ShapeDtypeStruct((rows, chans), f32),
            jax.ShapeDtypeStruct((rows, chans), f32),
            jax.ShapeDtypeStruct((modes, CHUNKS, chans), f32),
            pltpu.VMEM((modes + 16, chans), f32),
        ),
        in_specs=[pl.BlockSpec(memory_space=pltpu.VMEM)] * 5,
        out_specs=(pl.BlockSpec(memory_space=pltpu.VMEM),) * 4,
        scratch_shapes=[pltpu.VMEM((rows + 8, chans), f32), pltpu.VMEM((rows, chans), f32)],
        name="first_pass",
    )(query_proj, key_proj, value_proj, short_filter, decay_rate)

    def join(value, axis, lower, span):
        other = moved(value, axis, [(0, 1), (1, 0)])
        return pl.pallas_call(
            partial(joined, axis=axis, lower=lower, span=span),
            out_shape=(
                pltpu.VMEM((modes + 16, chans), f32),
                pltpu.VMEM((modes, chans), f32),
                pltpu.VMEM((8, chans), f32),
            ),
            in_specs=[pl.BlockSpec(memory_space=pltpu.VMEM)] * 4,
            out_specs=(pl.BlockSpec(memory_space=pltpu.VMEM),) * 3,
        )(decay_rate, short_filter, near_vmem(value), near_vmem(other))

    message, low, fix_low = join(message, "core", (), rows)
    message, mid, fix_mid = join(message, "xb", ("core",), rows * ncore)
    own, high, fix_high = join(message, "xa", ("xb", "core"), rows * ncore * lax.axis_size("xb"))
    back = {}
    back[1] = moved(own, "w", [(i, i + 1) for i in range(nw - 1)])
    back[3] = moved(own, "w", [(0, nw - 1)])
    nx = lax.axis_size(X)
    pieces = [weights] + [
        moved(weights, X, [(i, (i + d) % nx) for i in range(nx)]) for d in (2, 1, 3)
    ]
    pieces = [pieces[0], pieces[2], pieces[1], pieces[3]]
    held = jnp.where(lax.axis_index("w") == nw - 1, back[3], back[1])
    back[2] = moved(held, "w", [(nw - 2, nw - 1), (nw - 1, nw - 2)])
    gated = pl.pallas_call(
        second_pass,
        out_shape=jax.ShapeDtypeStruct((rows, chans), jnp.bfloat16),
        scratch_shapes=[pltpu.VMEM((rows, chans), f32), pltpu.VMEM((rows, chans), f32)],
        in_specs=[pl.BlockSpec(memory_space=pltpu.VMEM)] * 17,
        out_specs=pl.BlockSpec(memory_space=pltpu.VMEM),
        name="second_pass",
    )(
        featq, product, prefix, *[near_vmem(v) for v in (low, mid, high, fix_low, fix_mid, fix_high, own)],
        *[near_vmem(back[d]) for d in (1, 2, 3)],
        short_filter, decay_rate, residue, skip_gain[None],
    )
    quarter = rows // nb
    mine = lax.all_to_all(gated.reshape(nb, quarter, chans), "zb", 0, 0, tiled=True)
    *pieces, mine = lax.optimization_barrier((*pieces, mine))
    weights = jnp.stack(pieces, 0)
    other = moved(weights, "core", [(0, 1), (1, 0)])
    ny = lax.axis_size("y")
    copies = near_vmem(jnp.broadcast_to(mine[None], (ny,) + mine.shape))
    gathered = lax.all_to_all(copies, "y", 0, 0, tiled=True)
    shares = pl.pallas_call(
        project,
        out_shape=jax.ShapeDtypeStruct((na * nb, quarter, chans), jnp.bfloat16),
        in_specs=[
            pl.BlockSpec(memory_space=pltpu.VMEM),
            pl.BlockSpec(memory_space=pl.ANY),
            pl.BlockSpec(memory_space=pl.ANY),
        ],
        out_specs=pl.BlockSpec(memory_space=pltpu.VMEM),
        scratch_shapes=[
            pltpu.VMEM((nx, ncore) + weights.shape[1:], jnp.bfloat16),
            pltpu.SemaphoreType.DMA((2 * nx,)),
        ],
        name="project",
    )(gathered, weights, other)
    parts = lax.all_to_all(shares, ("za", "zb"), 0, 0, tiled=True)
    total = parts.reshape(na, rows, chans).astype(f32).sum(0)
    return total.astype(jnp.bfloat16)


def solution(mesh):
    fine = Mesh(mesh.devices.reshape(4, 2, 4, 4, 2, 2, 2), ("y", "za", "zb") + CTX)
    chan = ("y", "za", "zb")
    placed = (
        P(CTX, chan),
        P(CTX, chan),
        P(CTX, chan),
        P(None, None, chan),
        P(None, chan),
        P(None, chan),
        P(chan),
        P(chan, None),
    )
    return jax.shard_map(layer, mesh=fine, in_specs=placed, out_specs=P(CTX, chan), check_vma=False)
```

```python
from functools import partial

import jax
import jax.numpy as jnp
from jax import lax
from jax.experimental import pallas as pl
from jax.experimental.pallas import tpu as pltpu
from jax.sharding import Mesh, PartitionSpec as P


CTX = ("w", "xa", "xb", "core")
X = ("xa", "xb")
CHUNKS = 8


def features(padded, ref, taps):
    rows = ref.shape[0]
    padded[0:8, :] = jnp.zeros((8, ref.shape[1]), jnp.float32)
    padded[8:, :] = ref[...].astype(jnp.float32)
    total = taps[0:1, :] * padded[8 : 8 + rows, :]
    total = total + taps[1:2, :] * padded[7 : 7 + rows, :]
    return total + taps[2:3, :] * padded[6 : 6 + rows, :]


def first_pass(q, k, v, taps, rates, featq, product, prefix, message, padded, signal):
    rows, chans = q.shape
    length = rows // CHUNKS
    modes = rates.shape[0]
    weights = taps[...].astype(jnp.float32)
    featq[...] = features(padded, q, weights[0])
    last_query = padded[rows + 6 :, :]
    keyed = features(padded, k, weights[1])
    last_key = padded[rows + 6 :, :]
    valued = features(padded, v, weights[2])
    last_value = padded[rows + 6 :, :]
    edges = [keyed[0:2, :], valued[0:2, :], last_key, last_value, last_query]
    edges.append(jnp.zeros((6, chans), jnp.float32))
    prod = (keyed * valued).astype(jnp.bfloat16).astype(jnp.float32)
    product[...] = prod
    signal[...] = prod
    decay = [
        jnp.broadcast_to(jnp.exp(-rates[m : m + 1, :]), (CHUNKS, chans)) for m in range(modes)
    ]

    def step(t, held):
        row = signal[pl.ds(t, CHUNKS, stride=length), :]
        return tuple(decay[m] * held[m] + row for m in range(modes))

    zero = jnp.zeros((CHUNKS, chans), jnp.float32)
    held = lax.fori_loop(0, length, step, (zero,) * modes, unroll=4)
    index = lax.broadcasted_iota(jnp.int32, (CHUNKS, chans), 0)
    left = []
    for m in range(modes):
        rate = rates[m : m + 1, :]
        run = held[m]
        reach = 1
        while reach < CHUNKS:
            before = jnp.where(index >= reach, pltpu.roll(run, reach, 0), 0.0)
            run = run + jnp.exp(-rate * float(length * reach)) * before
            reach *= 2
        prefix[m] = jnp.where(index >= 1, pltpu.roll(run, 1, 0), 0.0)
        left.append(run[CHUNKS - 1 :, :])
    message[...] = jnp.concatenate(left + edges, axis=0)


def joined(rates, taps, own, other, out, before, fix, *, axis, lower, span):
    modes = rates.shape[0]
    rate = rates[...]
    right_side = lax.axis_index(axis) == 1
    left = jnp.where(right_side, other[...], own[...])
    right = jnp.where(right_side, own[...], other[...])
    first, second = edge_change(right, left, taps[...].astype(jnp.float32), modes)
    total = jnp.exp(-rate * float(span)) * left[0:modes, :] + right[0:modes, :]
    total = total + jnp.exp(-rate * (span - 1.0)) * first
    total = total + jnp.exp(-rate * (span - 2.0)) * second
    row = lax.broadcasted_iota(jnp.int32, left.shape, 0)
    edges = jnp.where(row < modes + 4, left, right)
    out[...] = jnp.concatenate([total, edges[modes:, :]], axis=0)
    inside = sum((lax.axis_index(a) for a in lower), jnp.int32(0))
    lost = jnp.exp(rate) * first + jnp.exp(2.0 * rate) * second
    lost = jnp.where(inside > 0, lost, 0.0)
    before[...] = jnp.where(right_side, left[0:modes, :] + lost, 0.0)
    rows = [first, second, left[modes + 8 : modes + 10, :]]
    rows.append(jnp.zeros((4,) + first.shape[1:], jnp.float32))
    leads = jnp.logical_and(right_side, inside == 0)
    fix[...] = jnp.where(leads, jnp.concatenate(rows, axis=0), 0.0)


def edge_change(message, before, taps, modes):
    def pair(head, tail, weights):
        old0 = message[modes + head : modes + head + 1, :]
        old1 = message[modes + head + 1 : modes + head + 2, :]
        back2 = before[modes + tail : modes + tail + 1, :]
        back1 = before[modes + tail + 1 : modes + tail + 2, :]
        new0 = (old0 + weights[1:2, :] * back1) + weights[2:3, :] * back2
        return old0, old1, new0, old1 + weights[2:3, :] * back1

    def rounded(value):
        return value.astype(jnp.bfloat16).astype(jnp.float32)

    k0, k1, kn0, kn1 = pair(0, 4, taps[1])
    v0, v1, vn0, vn1 = pair(2, 6, taps[2])
    return rounded(kn0 * vn0) - rounded(k0 * v0), rounded(kn1 * vn1) - rounded(k1 * v1)


def second_pass(
    featq, product, prefix, low, mid, high, fix_low, fix_mid, fix_high,
    own, back1, back2, back3,
    taps, rates, residue, gain, gated, signal, mixed,
):
    rows, chans = product.shape
    length = rows // CHUNKS
    modes = rates.shape[0]
    core, xb, xa = (lax.axis_index(a) for a in ("core", "xb", "xa"))
    two = rows * lax.axis_size("core")
    four = two * lax.axis_size("xb")
    run = four * lax.axis_size("xa")
    rate = rates[...]
    weights = taps[...].astype(jnp.float32)

    def power(tokens):
        return jnp.exp(-rate * tokens)

    chain = [own[...], back1[...], back2[...], back3[...], jnp.zeros(own.shape, jnp.float32)]
    start = jnp.zeros((modes, chans), jnp.float32)
    whole = power(float(run))
    for d in (3, 2, 1):
        first, second = edge_change(chain[d], chain[d + 1], weights, modes)
        total = chain[d][0:modes, :] + power(run - 1.0) * first + power(run - 2.0) * second
        start = whole * start + total
    first, second = edge_change(chain[0], chain[1], weights, modes)
    lost = jnp.exp(rate) * first + jnp.exp(2.0 * rate) * second
    ahead = (core * rows + xb * two + xa * four).astype(jnp.float32)
    leads = ahead < 1.0
    carried = start + jnp.where(leads, 0.0, lost)
    for part, place, span in ((high, xa, four), (mid, xb, two), (low, core, rows)):
        carried = part[...] + power(place.astype(jnp.float32) * float(span)) * carried
    far = jnp.concatenate([first, second, back1[modes + 8 : modes + 10, :]], axis=0)
    fix = fix_low[...] + fix_mid[...] + fix_high[...]
    fix = fix[0:4, :] + jnp.where(leads, far, 0.0)
    dp0, dp1, last2, last1 = (fix[i : i + 1, :] for i in range(4))
    lost = jnp.exp(rate) * dp0 + jnp.exp(2.0 * rate) * dp1

    wide = (CHUNKS, chans)
    row = lax.broadcasted_iota(jnp.int32, wide, 0)
    index = row.astype(jnp.float32)
    signal[...] = product[...]
    signal[0:CHUNKS, :] = product[0:CHUNKS, :] + jnp.where(
        row == 0, dp0, jnp.where(row == 1, dp1, 0.0)
    )
    held = []
    decay = []
    weight = []
    for m in range(modes):
        one = rate[m : m + 1, :]
        decay.append(jnp.broadcast_to(jnp.exp(-one), wide))
        weight.append(jnp.broadcast_to(residue[m : m + 1, :], wide))
        reach = jnp.exp(-one * (index * float(length)))
        before = carried[m : m + 1, :] + jnp.where(row >= 1, lost[m : m + 1, :], 0.0)
        held.append(prefix[m] + reach * before)

    def step(t, held):
        now = signal[pl.ds(t, CHUNKS, stride=length), :]
        held = tuple(decay[m] * held[m] + now for m in range(modes))
        terms = [weight[m] * held[m] for m in range(modes)]
        while len(terms) > 1:
            terms = [terms[i] + terms[i + 1] for i in range(0, len(terms), 2)]
        mixed[pl.ds(t, CHUNKS, stride=length), :] = terms[0]
        return held

    lax.fori_loop(0, length, step, tuple(held), unroll=2)
    long_out = (mixed[...] + gain[...] * signal[...]).astype(jnp.bfloat16).astype(jnp.float32)
    gated[...] = (featq[...] * long_out).astype(jnp.bfloat16)
    top = lax.broadcasted_iota(jnp.int32, (16, chans), 0)
    dq0 = weights[0][1:2, :] * last1 + weights[0][2:3, :] * last2
    dq1 = weights[0][2:3, :] * last1
    query = featq[0:16, :] + jnp.where(top == 0, dq0, jnp.where(top == 1, dq1, 0.0))
    gated[0:16, :] = (query * long_out[0:16, :]).astype(jnp.bfloat16)


def project(gathered, mine, other, shares):
    ny, nb = gathered.shape[:2]
    nx = mine.shape[0]
    core = lax.axis_index("core")
    width = shares.shape[2]

    def run(halves):
        left = jnp.concatenate([gathered[i, j] for i in range(ny) for j in range(nb)], axis=1)
        for n in range(0, shares.shape[0], 2):
            cols = slice(n * width, (n + 2) * width)
            right = jnp.concatenate(
                [
                    half[x, i, j, :, cols]
                    for i in range(ny)
                    for j in range(nb)
                    for x in range(nx)
                    for half in halves
                ],
                axis=0,
            )
            both = jnp.dot(left, right, preferred_element_type=jnp.float32).astype(shares.dtype)
            shares[n] = both[:, :width]
            shares[n + 1] = both[:, width:]

    @pl.when(core == 0)
    def _():
        run((mine, other))

    @pl.when(core == 1)
    def _():
        run((other, mine))


def moved(value, axis, pairs):
    return lax.ppermute(value, axis, pairs)


def near_vmem(value):
    return pltpu.with_memory_space_constraint(value, pltpu.VMEM)


def everyone(value, axis):
    count = lax.axis_size(axis)
    return lax.all_to_all(
        jnp.broadcast_to(value[None], (count,) + value.shape), axis, 0, 0, tiled=True
    )


def own_weights(out_weight):
    ny, nb = lax.axis_size("y"), lax.axis_size("zb")
    ncore = lax.axis_size("core")
    share = out_weight.shape[0] // (lax.axis_size(X) * ncore)
    first = (lax.axis_index(X) * ncore + lax.axis_index("core")) * share
    rows = lax.dynamic_slice_in_dim(out_weight, first, share, 0)
    blocks = rows.reshape(share, ny, -1).transpose(1, 0, 2)
    blocks = jnp.broadcast_to(blocks[:, None], (ny, nb) + blocks.shape[1:])
    blocks = blocks.reshape((ny * nb,) + blocks.shape[2:])
    got = lax.all_to_all(blocks, ("y", "zb"), 0, 0, tiled=True)
    return got.reshape((ny, nb) + got.shape[1:])


def layer(
    key_proj, value_proj, query_proj, short_filter, decay_rate, residue, skip_gain, out_weight
):
    rows, chans = key_proj.shape
    modes = decay_rate.shape[0]
    na, nb = lax.axis_size("za"), lax.axis_size("zb")
    ncore, nw = lax.axis_size("core"), lax.axis_size("w")
    f32 = jnp.float32
    weights = own_weights(out_weight)
    featq, product, prefix, message = pl.pallas_call(
        first_pass,
        out_shape=(
            jax.ShapeDtypeStruct((rows, chans), f32),
            jax.ShapeDtypeStruct((rows, chans), f32),
            jax.ShapeDtypeStruct((modes, CHUNKS, chans), f32),
            pltpu.VMEM((modes + 16, chans), f32),
        ),
        in_specs=[pl.BlockSpec(memory_space=pltpu.VMEM)] * 5,
        out_specs=(pl.BlockSpec(memory_space=pltpu.VMEM),) * 4,
        scratch_shapes=[pltpu.VMEM((rows + 8, chans), f32), pltpu.VMEM((rows, chans), f32)],
        name="first_pass",
    )(query_proj, key_proj, value_proj, short_filter, decay_rate)

    def join(value, axis, lower, span):
        other = moved(value, axis, [(0, 1), (1, 0)])
        return pl.pallas_call(
            partial(joined, axis=axis, lower=lower, span=span),
            out_shape=(
                pltpu.VMEM((modes + 16, chans), f32),
                pltpu.VMEM((modes, chans), f32),
                pltpu.VMEM((8, chans), f32),
            ),
            in_specs=[pl.BlockSpec(memory_space=pltpu.VMEM)] * 4,
            out_specs=(pl.BlockSpec(memory_space=pltpu.VMEM),) * 3,
        )(decay_rate, short_filter, near_vmem(value), near_vmem(other))

    message, low, fix_low = join(message, "core", (), rows)
    message, mid, fix_mid = join(message, "xb", ("core",), rows * ncore)
    own, high, fix_high = join(message, "xa", ("xb", "core"), rows * ncore * lax.axis_size("xb"))
    back = {}
    back[1] = moved(own, "w", [(i, i + 1) for i in range(nw - 1)])
    back[3] = moved(own, "w", [(0, nw - 1)])
    weights = everyone(weights, X)
    held = jnp.where(lax.axis_index("w") == nw - 1, back[3], back[1])
    back[2] = moved(held, "w", [(nw - 2, nw - 1), (nw - 1, nw - 2)])
    gated = pl.pallas_call(
        second_pass,
        out_shape=jax.ShapeDtypeStruct((rows, chans), jnp.bfloat16),
        scratch_shapes=[pltpu.VMEM((rows, chans), f32), pltpu.VMEM((rows, chans), f32)],
        in_specs=[pl.BlockSpec(memory_space=pltpu.VMEM)] * 17,
        out_specs=pl.BlockSpec(memory_space=pltpu.VMEM),
        name="second_pass",
    )(
        featq, product, prefix, *[near_vmem(v) for v in (low, mid, high, fix_low, fix_mid, fix_high, own)],
        *[near_vmem(back[d]) for d in (1, 2, 3)],
        short_filter, decay_rate, residue, skip_gain[None],
    )
    other = moved(weights, "core", [(0, 1), (1, 0)])
    quarter = rows // nb
    mine = lax.all_to_all(gated.reshape(nb, quarter, chans), "zb", 0, 0, tiled=True)
    ny = lax.axis_size("y")
    copies = near_vmem(jnp.broadcast_to(mine[None], (ny,) + mine.shape))
    gathered = lax.all_to_all(copies, "y", 0, 0, tiled=True)
    shares = pl.pallas_call(
        project,
        out_shape=jax.ShapeDtypeStruct((na * nb, quarter, chans), jnp.bfloat16),
        name="project",
    )(gathered, weights, other)
    parts = lax.all_to_all(shares, ("za", "zb"), 0, 0, tiled=True)
    total = parts.reshape(na, rows, chans).astype(f32).sum(0)
    return total.astype(jnp.bfloat16)


def solution(mesh):
    fine = Mesh(mesh.devices.reshape(4, 2, 4, 4, 2, 2, 2), ("y", "za", "zb") + CTX)
    chan = ("y", "za", "zb")
    placed = (
        P(CTX, chan),
        P(CTX, chan),
        P(CTX, chan),
        P(None, None, chan),
        P(None, chan),
        P(None, chan),
        P(chan),
        P(chan, None),
    )
    return jax.shard_map(layer, mesh=fine, in_specs=placed, out_specs=P(CTX, chan), check_vma=False)
```
